32 devices in a mesh: row: 4 (over z), col: 8 (over y, x, core).
Axes of the slice: x: 2, y: 2, z: 4, core: 2. Of those that a mesh axis runs over, the one named last changes fastest.
Arguments:
- diag_inverse: float32 [1024, 1024], P(('row', 'col')), as said below
- row_basis: float32 [16, 128, 1024], P('row', 'col'), may hold values from -6 to 6
- row_coef: float32 [16, 128, 1024], P('row', 'col'), may hold values from -0.09375 to 0.09375
- row_ranks: int32 [16], P('row'), may hold values from 16 to 128, as said below
- col_basis: float32 [24, 128, 1024], P('col', 'row'), may hold values from -6 to 6
- col_coef: float32 [24, 128, 1024], P('col', 'row'), may hold values from -0.09375 to 0.09375
- col_ranks: int32 [24], P('col'), may hold values from 16 to 128, as said below
- tile_basis: float32 [16, 24, 1024, 128], P('row', 'col'), may hold values from -6 to 6
- tile_coef: float32 [16, 24, 1024, 128], P('row', 'col'), may hold values from -0.5 to 0.5
- tile_ranks: int32 [16, 24], P('row', 'col'), may hold values from 16 to 128, as said below
Outputs:
- new_basis: bfloat16 [16, 24, 1024, 128], P('row', 'col')
- new_coef: bfloat16 [16, 24, 1024, 128], P('row', 'col')
The draws below stay inside these ranges and needn't reach their ends.
Inputs may be any that keep to these rules, and one draw needn't show every extreme that they name: `row_ranks`: rank of each panel tile; the smallest and largest values occur in every draw. `col_ranks`: rank of each panel tile; the smallest and largest values occur in every draw. `tile_ranks`: rank of each trailing tile; the smallest and largest values occur in every draw. `diag_inverse`: lower triangular with a positive diagonal.
All inputs are finite; a program needn't handle non-finite values.
Results may differ from the reference program's by a relative error of at most 0.001.
Values sent between devices are 32-bit elements; how exact they have to be, the bound alone decides.
A program may use at most 128 MiB of HBM per device.

```python
import math
import jax
import jax.numpy as jnp
from jax import lax

NB = 1024
RMAX = 128
RLOW = 16
NR = 16
NC = 24


def pick_ranks(key, array_shape):
    tile_count = 1
    for extent in array_shape:
        tile_count = tile_count * extent
    values = jax.random.randint(key, (tile_count,), RLOW, RMAX + 1)
    top_slot = jax.random.randint(jax.random.fold_in(key, 1), (), 0, tile_count)
    offset = jax.random.randint(jax.random.fold_in(key, 2), (), 1, tile_count)
    second = (top_slot + offset) % tile_count
    slot_ids = jnp.arange(tile_count)
    values = jnp.where(slot_ids == top_slot, RMAX, values)
    values = jnp.where(slot_ids == second, RLOW, values)
    return values.reshape(array_shape).astype(jnp.int32)


def draw_row_ranks(key, part):
    return pick_ranks(jax.random.fold_in(key, 11), (NR,))


def draw_col_ranks(key, part):
    return pick_ranks(jax.random.fold_in(key, 23), (NC,))


def draw_tile_ranks(key, part):
    return pick_ranks(jax.random.fold_in(key, 37), (NR, NC))


def draw_diag_inverse(key, part):
    seeded = jax.random.fold_in(key, 41)
    lower_part = jax.random.normal(seeded, (NB, NB), jnp.float32)
    diagonal_part = jax.random.uniform(jax.random.fold_in(key, 43), (NB,), jnp.float32, 1.0, 2.0)
    row_ids = jnp.arange(NB, dtype=jnp.int32)[:, None]
    col_ids = jnp.arange(NB, dtype=jnp.int32)[None, :]
    below = jnp.where(row_ids > col_ids, lower_part * (1.0 / NB ** 0.5), 0.0)
    return below + jnp.where(row_ids == col_ids, diagonal_part[:, None], 0.0)


def steps_of(own_key, shape, pieces, smallest, largest):
    def one(axis_at, shards_of):
        steps = jax.random.uniform(jax.random.fold_in(jax.random.fold_in(own_key, 6), axis_at), (shards_of,), jnp.float32, smallest / len(pieces), largest / len(pieces))
        return jnp.repeat(jnp.exp(steps), shape[axis_at] // shards_of).reshape((-1,) + (1,) * (len(shape) - axis_at - 1))

    loudness = one(*pieces[0])
    for cut in pieces[1:]:
        loudness = loudness * one(*cut)
    return loudness


def bell_draw(stream_key, dims, deviation, reach, cuts=(), held_as=jnp.bfloat16):
    gain = steps_of(stream_key, dims, cuts, -0.22, 0.18) if cuts else 1.0
    entries = jax.random.normal(stream_key, dims, jnp.float32) * deviation * gain
    return jnp.minimum(jnp.maximum(entries, -reach), reach).astype(held_as)


def setup_inputs(seed: int = 0) -> dict:
    key_list = jax.random.split(jax.random.key(seed), 11)
    return {
        "diag_inverse": draw_diag_inverse(jax.random.fold_in(key_list[10], 71), 0),
        "row_basis": bell_draw(key_list[1], (NR, RMAX, NB), 1.0, 6.0, ((0, 4), (1, 8)), jnp.float32),
        "row_coef": bell_draw(key_list[2], (NR, RMAX, NB), (RMAX * 32) ** -0.5, 0.09375, ((0, 4), (1, 8)), jnp.float32),
        "row_ranks": draw_row_ranks(jax.random.fold_in(key_list[10], 71), 0),
        "col_basis": bell_draw(key_list[4], (NC, RMAX, NB), 1.0, 6.0, ((0, 8), (1, 4)), jnp.float32),
        "col_coef": bell_draw(key_list[5], (NC, RMAX, NB), (RMAX * 32) ** -0.5, 0.09375, ((0, 8), (1, 4)), jnp.float32),
        "col_ranks": draw_col_ranks(jax.random.fold_in(key_list[10], 71), 0),
        "tile_basis": bell_draw(key_list[7], (NR, NC, NB, RMAX), 1.0, 6.0, ((0, 4), (1, 8)), jnp.float32),
        "tile_coef": bell_draw(key_list[8], (NR, NC, NB, RMAX), RMAX ** -0.5, 0.5, ((0, 4), (1, 8)), jnp.float32),
        "tile_ranks": draw_tile_ranks(jax.random.fold_in(key_list[10], 71), 0),
    }


HIGHEST = lax.Precision.HIGHEST

def orthonormal(sketch_block, rank_keep):
    gram_matrix = jnp.dot(sketch_block.T, sketch_block, precision=HIGHEST) + jnp.diag(1.0 - rank_keep)
    factor = jnp.linalg.cholesky(gram_matrix)
    return jax.scipy.linalg.solve_triangular(factor, sketch_block.T, lower=True).T

def recompress(tile_left, tile_right, rank_keep, left_panel, coupling, right_panel):
    tile_left = tile_left * rank_keep[None, :]
    tile_right = tile_right * rank_keep[None, :]
    inner_gram = jnp.dot(tile_right.T, tile_right, precision=HIGHEST)
    cross_term = jnp.dot(right_panel, tile_right, precision=HIGHEST)
    sketch = jnp.dot(tile_left, inner_gram, precision=HIGHEST) - jnp.dot(left_panel.T, jnp.dot(coupling, cross_term, precision=HIGHEST), precision=HIGHEST)
    ortho_basis = orthonormal(orthonormal(sketch, rank_keep), rank_keep)
    first_part = jnp.dot(tile_right, jnp.dot(tile_left.T, ortho_basis, precision=HIGHEST), precision=HIGHEST)
    left_proj = jnp.dot(left_panel, ortho_basis, precision=HIGHEST)
    second_part = jnp.dot(right_panel.T, jnp.dot(coupling.T, left_proj, precision=HIGHEST), precision=HIGHEST)
    scaled_basis = ortho_basis * math.sqrt(ortho_basis.shape[0])
    return (scaled_basis.astype(jnp.bfloat16), (first_part - second_part).astype(jnp.bfloat16))

def panel_factors(basis_rows, coef_rows, panel_ranks, inverse_factor):
    rank_keep = (jnp.arange(RMAX, dtype=jnp.int32)[None, :] < panel_ranks[:, None]).astype(jnp.float32)[:, :, None]
    basis_rows = basis_rows * rank_keep
    coef_rows = coef_rows * rank_keep
    tile_count = coef_rows.shape[0]
    flat_rows = coef_rows.reshape(tile_count * RMAX, NB)
    solved = jnp.dot(flat_rows, inverse_factor.T, precision=HIGHEST)
    return (basis_rows, solved.reshape(tile_count, RMAX, NB))

def reference(diag_inverse, row_basis, row_coef, row_ranks, col_basis, col_coef, col_ranks, tile_basis, tile_coef, tile_ranks):
    row_left, row_solved = panel_factors(row_basis, row_coef, row_ranks, diag_inverse)
    col_left, col_solved = panel_factors(col_basis, col_coef, col_ranks, diag_inverse)

    def one_tile(position):
        tile_row = position // NC
        tile_col = position % NC
        coupling = jnp.dot(row_solved[tile_row], col_solved[tile_col].T, precision=HIGHEST)
        rank_keep = (jnp.arange(RMAX, dtype=jnp.int32) < tile_ranks[tile_row, tile_col]).astype(jnp.float32)
        return recompress(tile_basis[tile_row, tile_col], tile_coef[tile_row, tile_col], rank_keep, row_left[tile_row], coupling, col_left[tile_col])
    out_basis, out_coef = lax.map(one_tile, jnp.arange(NR * NC, dtype=jnp.int32))
    return (out_basis.reshape(NR, NC, NB, RMAX), out_coef.reshape(NR, NC, NB, RMAX))
```

```python
import math

import jax
import jax.numpy as jnp
from jax import lax
from jax.experimental import pallas as pl
from jax.experimental.pallas import tpu as pltpu
from jax.sharding import PartitionSpec as P

HIGHEST = lax.Precision.HIGHEST


HIGH = lax.Precision.HIGH
PIVOT_ROWS = 32


def batch_dot(left, right, left_dim, right_dim):
    dims = (((left_dim,), (right_dim,)), ((), ()))
    return lax.dot_general(
        left, right, dims, precision=HIGHEST, preferred_element_type=jnp.float32
    )


def factor_inverse_into(work_ref, tile_count, width):
    rows = PIVOT_ROWS
    lane_half = width // 2
    row_ids = lax.broadcasted_iota(jnp.int32, (1, rows, 1), 1)
    eye_lane = (
        lax.broadcasted_iota(jnp.int32, (1, rows, width), 1)
        == lax.broadcasted_iota(jnp.int32, (1, rows, width), 2)
    ).astype(jnp.float32)
    pick_row = lax.broadcasted_iota(jnp.int32, (width, width), 0)
    pick_lane = lax.broadcasted_iota(jnp.int32, (width, width), 1)
    lane_ids = lax.broadcasted_iota(jnp.int32, (rows, width), 1)

    def block_step(block, carry):
        start = pl.multiple_of(block * rows, rows)
        picker = jnp.where(
            (pick_lane >= lane_half)
            & (pick_lane < lane_half + rows)
            & (pick_row == start + pick_lane - lane_half),
            1.0,
            0.0,
        )
        strip = work_ref[:, pl.ds(start, rows), :width].reshape(tile_count * rows, width)
        state = batch_dot(strip, picker, 1, 0).reshape(tile_count, rows, width) + eye_lane
        pivots = jnp.zeros((tile_count, rows, 1), jnp.float32)
        for j in range(rows):
            column = state[:, :, lane_half + j : lane_half + j + 1]
            pivot = column[:, j : j + 1, :]
            pivots = jnp.where(row_ids == j, pivot, pivots)
            if j < rows - 1:
                multiplier = jnp.where(row_ids > j, column / pivot, 0.0)
                state = state - multiplier * state[:, j : j + 1, :]
        state = state * (1.0 / jnp.sqrt(pivots))
        for t in range(tile_count):
            solved = batch_dot(state[t, :, :rows], work_ref[t, pl.ds(start, rows), :], 1, 0)
            below = jnp.where(lane_ids >= start + rows, solved[:, :width], 0.0)
            work_ref[t] = work_ref[t] - batch_dot(below, solved, 0, 0)
            work_ref[t, pl.ds(start, rows), :] = solved
        return carry

    lax.fori_loop(0, width // rows, block_step, 0)


def twice_kernel(gram_ref, out_ref, work_ref):
    tile_count, width, _ = gram_ref.shape
    eye = (
        lax.broadcasted_iota(jnp.int32, (width, width), 0)
        == lax.broadcasted_iota(jnp.int32, (width, width), 1)
    ).astype(jnp.float32)
    for t in range(tile_count):
        out_ref[t] = eye

    def one_pass(step, carry):
        for t in range(tile_count):
            inverse = out_ref[t]
            again = batch_dot(inverse, batch_dot(gram_ref[t], inverse, 1, 1), 1, 0)
            work_ref[t, :, :width] = 0.5 * (again + again.T)
            work_ref[t, :, width:] = eye
        factor_inverse_into(work_ref, tile_count, width)
        for t in range(tile_count):
            out_ref[t] = batch_dot(work_ref[t, :, width:], out_ref[t], 1, 0)
        return carry

    lax.fori_loop(0, 2, one_pass, 0)


def combined_inverse(gram_matrix):
    tile_count, width, _ = gram_matrix.shape
    return pl.pallas_call(
        twice_kernel,
        out_shape=jax.ShapeDtypeStruct(gram_matrix.shape, jnp.float32),
        in_specs=[pl.BlockSpec(memory_space=pltpu.VMEM)],
        out_specs=pl.BlockSpec(memory_space=pltpu.VMEM),
        scratch_shapes=[pltpu.VMEM((tile_count, width, 2 * width), jnp.float32)],
        name="factor_twice",
    )(gram_matrix)


def orthonormal_twice(sketch_block, rank_keep):
    rank_width = rank_keep.shape[-1]
    eye_one = jnp.eye(rank_width, dtype=jnp.float32)[None, :, :]
    gram_matrix = jnp.einsum("tnr,tns->trs", sketch_block, sketch_block, precision=HIGHEST)
    gram_matrix = gram_matrix + eye_one * (1.0 - rank_keep)[:, None, :]
    combined = combined_inverse(gram_matrix)
    return jnp.einsum("tnr,tsr->tns", sketch_block, combined, precision=HIGH)


def share_mask(panel_ranks, rank_share, position):
    columns = position * rank_share + jnp.arange(rank_share, dtype=jnp.int32)
    return (columns[None, :] < panel_ranks[:, None]).astype(jnp.float32)[:, :, None]


def solve_rows(inverse_factor, coef_rows):
    tile_count, rank_rows, order = coef_rows.shape
    flat_rows = coef_rows.reshape(tile_count * rank_rows, order)
    solved = jnp.dot(flat_rows, inverse_factor.T, precision=HIGHEST)
    return solved.reshape(tile_count, rank_rows, order)


def body(
    diag_inverse,
    row_basis,
    row_coef,
    row_ranks,
    col_basis,
    col_coef,
    col_ranks,
    tile_basis,
    tile_coef,
    tile_ranks,
):
    inverse_whole = lax.all_gather(diag_inverse, ("row", "col"), axis=0, tiled=True)
    row_keep = share_mask(row_ranks, row_basis.shape[1], lax.axis_index("col"))
    row_left = row_basis * row_keep
    row_send = row_coef * row_keep
    row_send = solve_rows(inverse_whole, row_send)
    row_left, row_solved = (
        lax.all_gather(row_left, "col", axis=1, tiled=True),
        lax.all_gather(row_send, "col", axis=1, tiled=True),
    )
    col_keep = share_mask(col_ranks, col_basis.shape[1], lax.axis_index("row"))
    col_left = col_basis * col_keep
    col_send = col_coef * col_keep
    col_send = solve_rows(inverse_whole, col_send)
    col_left, col_solved = (
        lax.all_gather(col_left, "row", axis=1, tiled=True),
        lax.all_gather(col_send, "row", axis=1, tiled=True),
    )
    local_rows, local_cols, order, rank_width = tile_basis.shape
    all_coupling = jnp.dot(
        row_solved.reshape(local_rows * rank_width, order),
        col_solved.reshape(local_cols * rank_width, order).T,
        precision=HIGH,
    )
    coupling = jnp.transpose(
        all_coupling.reshape(local_rows, rank_width, local_cols, rank_width), (0, 2, 1, 3)
    )
    tile_count = local_rows * local_cols
    rank_keep = (
        jnp.arange(rank_width, dtype=jnp.int32)[None, None, :] < tile_ranks[:, :, None]
    ).astype(jnp.float32)
    masked_left = tile_basis * rank_keep[:, :, None, :]
    masked_right = tile_coef * rank_keep[:, :, None, :]

    def make_sketch(tile_left, tile_right, left_panel, pair_coupling, right_panel):
        inner_gram = jnp.dot(tile_right.T, tile_right, precision=HIGH)
        cross_term = jnp.dot(right_panel, tile_right, precision=HIGH)
        return jnp.dot(tile_left, inner_gram, precision=HIGH) - jnp.dot(
            left_panel.T, jnp.dot(pair_coupling, cross_term, precision=HIGH), precision=HIGH
        )

    sketch_inner = jax.vmap(make_sketch, in_axes=(0, 0, None, 0, 0))
    sketch = jax.vmap(sketch_inner, in_axes=(0, 0, 0, 0, None))(
        masked_left, masked_right, row_left, coupling, col_left
    )
    flat_keep = rank_keep.reshape(tile_count, rank_width)
    flat_sketch = sketch.reshape(tile_count, order, rank_width)
    ortho_basis = orthonormal_twice(flat_sketch, flat_keep).reshape(
        local_rows, local_cols, order, rank_width
    )

    def make_coef(tile_left, tile_right, left_panel, pair_coupling, right_panel, basis_block):
        first_part = jnp.dot(
            tile_right, jnp.dot(tile_left.T, basis_block, precision=HIGH), precision=HIGH
        )
        left_proj = jnp.dot(left_panel, basis_block, precision=HIGH)
        second_part = jnp.dot(
            right_panel.T, jnp.dot(pair_coupling.T, left_proj, precision=HIGH), precision=HIGH
        )
        return first_part - second_part

    coef_inner = jax.vmap(make_coef, in_axes=(0, 0, None, 0, 0, 0))
    new_coef = jax.vmap(coef_inner, in_axes=(0, 0, 0, 0, None, 0))(
        masked_left, masked_right, row_left, coupling, col_left, ortho_basis
    )
    scaled_basis = ortho_basis * math.sqrt(order)
    return (scaled_basis.astype(jnp.bfloat16), new_coef.astype(jnp.bfloat16))


def solution(mesh):
    placed = (
        P(("row", "col"), None),
        P("row", "col", None),
        P("row", "col", None),
        P("row"),
        P("col", "row", None),
        P("col", "row", None),
        P("col"),
        P("row", "col", None, None),
        P("row", "col", None, None),
        P("row", "col"),
    )
    return jax.shard_map(
        body,
        mesh=mesh,
        in_specs=placed,
        out_specs=(P("row", "col", None, None), P("row", "col", None, None)),
        check_vma=False,
    )
```

```python
import math

import jax
import jax.numpy as jnp
from jax import lax
from jax.experimental import pallas as pl
from jax.experimental.pallas import tpu as pltpu
from jax.sharding import PartitionSpec as P

HIGHEST = lax.Precision.HIGHEST


HIGH = lax.Precision.HIGH
PIVOT_ROWS = 32


def batch_dot(left, right, left_dim, right_dim):
    dims = (((left_dim,), (right_dim,)), ((), ()))
    return lax.dot_general(
        left, right, dims, precision=HIGHEST, preferred_element_type=jnp.float32
    )


def plain_dot(left, right, left_dim, right_dim):
    dims = (((left_dim,), (right_dim,)), ((), ()))
    return lax.dot_general(left, right, dims, preferred_element_type=jnp.float32)


def split(values):
    high = values.astype(jnp.bfloat16)
    return high, (values - high.astype(jnp.float32)).astype(jnp.bfloat16)


def split_dot(left, right):
    left_high, left_low = split(left)
    right_high, right_low = split(right)
    return plain_dot(left_high, right_high, 1, 0) + (
        plain_dot(left_high, right_low, 1, 0) + plain_dot(left_low, right_high, 1, 0)
    )


def factor_inverse_into(work_ref, tile_count, width):
    rows = PIVOT_ROWS
    lane_half = width // 2
    sub_ids = lax.broadcasted_iota(jnp.int32, (1, 8, 1), 1)
    diag_lane = (
        lax.broadcasted_iota(jnp.int32, (1, rows, width), 1) + lane_half
        == lax.broadcasted_iota(jnp.int32, (1, rows, width), 2)
    )
    eye_lane = (
        lax.broadcasted_iota(jnp.int32, (1, rows, width), 1)
        == lax.broadcasted_iota(jnp.int32, (1, rows, width), 2)
    ).astype(jnp.float32)
    pick_row = lax.broadcasted_iota(jnp.int32, (width, width), 0)
    pick_lane = lax.broadcasted_iota(jnp.int32, (width, width), 1)
    lane_ids = lax.broadcasted_iota(jnp.int32, (rows, width), 1)

    def block_step(block, carry):
        start = pl.multiple_of(block * rows, rows)
        picker = jnp.where(
            (pick_lane >= lane_half)
            & (pick_lane < lane_half + rows)
            & (pick_row == start + pick_lane - lane_half),
            1.0,
            0.0,
        )
        strip = work_ref[:, pl.ds(start, rows), :width].reshape(tile_count * rows, width)
        state = batch_dot(strip, picker, 1, 0).reshape(tile_count, rows, width) + eye_lane
        groups = [state[:, g * 8 : g * 8 + 8, :] for g in range(rows // 8)]
        for j in range(rows - 1):
            own, inner = j // 8, j % 8
            lane = lane_half + j
            pivot_row = groups[own][:, inner : inner + 1, :]
            pivot_row = pivot_row * (1.0 / pivot_row[:, :, lane : lane + 1])
            for g in range(own, rows // 8):
                column = groups[g][:, :, lane : lane + 1]
                if g == own:
                    if inner == 7:
                        continue
                    column = jnp.where(sub_ids > inner, column, 0.0)
                groups[g] = groups[g] - column * pivot_row
        state = jnp.concatenate(groups, axis=1)
        pivots = jnp.sum(jnp.where(diag_lane, state, 0.0), axis=2, keepdims=True)
        state = state * (1.0 / jnp.sqrt(pivots))
        solved_all = []
        for t in range(tile_count):
            solved_all.append(split_dot(state[t, :, :rows], work_ref[t, pl.ds(start, rows), :]))
        for t in range(tile_count):
            right_high, right_low = split(solved_all[t])
            below = jnp.where(lane_ids >= start + rows, solved_all[t][:, :width], 0.0)
            left_high, left_low = split(below)
            left = jnp.concatenate([left_high, left_high, left_low], axis=0)
            right = jnp.concatenate([right_high, right_low, right_high], axis=0)
            work_ref[t] = work_ref[t] - plain_dot(left, right, 0, 0)
        for t in range(tile_count):
            work_ref[t, pl.ds(start, rows), :] = solved_all[t]
        return carry

    lax.fori_loop(0, width // rows, block_step, 0)


def twice_kernel(gram_ref, out_ref, work_ref):
    tile_count, width, _ = gram_ref.shape
    eye = (
        lax.broadcasted_iota(jnp.int32, (width, width), 0)
        == lax.broadcasted_iota(jnp.int32, (width, width), 1)
    ).astype(jnp.float32)
    for t in range(tile_count):
        out_ref[t] = eye

    def one_pass(step, carry):
        for t in range(tile_count):
            inverse = out_ref[t]
            again = batch_dot(inverse, batch_dot(gram_ref[t], inverse, 1, 1), 1, 0)
            work_ref[t, :, :width] = 0.5 * (again + again.T)
            work_ref[t, :, width:] = eye
        factor_inverse_into(work_ref, tile_count, width)
        for t in range(tile_count):
            out_ref[t] = batch_dot(work_ref[t, :, width:], out_ref[t], 1, 0)
        return carry

    lax.fori_loop(0, 2, one_pass, 0)


def combined_inverse(gram_matrix):
    tile_count, width, _ = gram_matrix.shape
    return pl.pallas_call(
        twice_kernel,
        out_shape=jax.ShapeDtypeStruct(gram_matrix.shape, jnp.float32),
        in_specs=[pl.BlockSpec(memory_space=pltpu.VMEM)],
        out_specs=pl.BlockSpec(memory_space=pltpu.VMEM),
        scratch_shapes=[pltpu.VMEM((tile_count, width, 2 * width), jnp.float32)],
        name="factor_twice",
    )(gram_matrix)


def orthonormal_twice(sketch_block, rank_keep):
    rank_width = rank_keep.shape[-1]
    eye_one = jnp.eye(rank_width, dtype=jnp.float32)[None, :, :]
    gram_matrix = jnp.einsum("tnr,tns->trs", sketch_block, sketch_block, precision=HIGHEST)
    gram_matrix = gram_matrix + eye_one * (1.0 - rank_keep)[:, None, :]
    combined = combined_inverse(gram_matrix)
    return jnp.einsum("tnr,tsr->tns", sketch_block, combined, precision=HIGH)


def share_mask(panel_ranks, rank_share, position):
    columns = position * rank_share + jnp.arange(rank_share, dtype=jnp.int32)
    return (columns[None, :] < panel_ranks[:, None]).astype(jnp.float32)[:, :, None]


def solve_rows(inverse_factor, coef_rows):
    tile_count, rank_rows, order = coef_rows.shape
    flat_rows = coef_rows.reshape(tile_count * rank_rows, order)
    solved = jnp.dot(flat_rows, inverse_factor.T, precision=HIGHEST)
    return solved.reshape(tile_count, rank_rows, order)


def rotated_gather(share, axis_name):
    count = lax.axis_size(axis_name)
    pieces = [share]
    for shift in range(1, count):
        pairs = [((i + shift) % count, i) for i in range(count)]
        pieces.append(lax.ppermute(share, axis_name, pairs))
    return jnp.concatenate(pieces, axis=1)


def body(
    diag_inverse,
    row_basis,
    row_coef,
    row_ranks,
    col_basis,
    col_coef,
    col_ranks,
    tile_basis,
    tile_coef,
    tile_ranks,
):
    inverse_whole = lax.all_gather(diag_inverse, ("row", "col"), axis=0, tiled=True)
    row_keep = share_mask(row_ranks, row_basis.shape[1], lax.axis_index("col"))
    col_keep = share_mask(col_ranks, col_basis.shape[1], lax.axis_index("row"))
    col_left = rotated_gather(col_basis * col_keep, "row")
    row_left = rotated_gather(row_basis * row_keep, "col")
    inverse_whole, col_left, row_left = lax.optimization_barrier(
        (inverse_whole, col_left, row_left)
    )
    row_solved = rotated_gather(solve_rows(inverse_whole, row_coef * row_keep), "col")
    col_solved = rotated_gather(solve_rows(inverse_whole, col_coef * col_keep), "row")
    local_rows, local_cols, order, rank_width = tile_basis.shape
    all_coupling = jnp.dot(
        row_solved.reshape(local_rows * rank_width, order),
        col_solved.reshape(local_cols * rank_width, order).T,
        precision=HIGH,
    )
    coupling = jnp.transpose(
        all_coupling.reshape(local_rows, rank_width, local_cols, rank_width), (0, 2, 1, 3)
    )
    tile_count = local_rows * local_cols
    rank_keep = (
        jnp.arange(rank_width, dtype=jnp.int32)[None, None, :] < tile_ranks[:, :, None]
    ).astype(jnp.float32)
    masked_left = tile_basis * rank_keep[:, :, None, :]
    masked_right = tile_coef * rank_keep[:, :, None, :]

    def make_sketch(tile_left, tile_right, left_panel, pair_coupling, right_panel):
        inner_gram = jnp.dot(tile_right.T, tile_right, precision=HIGH)
        cross_term = jnp.dot(right_panel, tile_right, precision=HIGH)
        return jnp.dot(tile_left, inner_gram, precision=HIGH) - jnp.dot(
            left_panel.T, jnp.dot(pair_coupling, cross_term, precision=HIGH), precision=HIGH
        )

    sketch_inner = jax.vmap(make_sketch, in_axes=(0, 0, None, 0, 0))
    sketch = jax.vmap(sketch_inner, in_axes=(0, 0, 0, 0, None))(
        masked_left, masked_right, row_left, coupling, col_left
    )
    flat_keep = rank_keep.reshape(tile_count, rank_width)
    flat_sketch = sketch.reshape(tile_count, order, rank_width)
    ortho_basis = orthonormal_twice(flat_sketch, flat_keep).reshape(
        local_rows, local_cols, order, rank_width
    )

    def make_coef(tile_left, tile_right, left_panel, pair_coupling, right_panel, basis_block):
        first_part = jnp.dot(
            tile_right, jnp.dot(tile_left.T, basis_block, precision=HIGH), precision=HIGH
        )
        left_proj = jnp.dot(left_panel, basis_block, precision=HIGH)
        second_part = jnp.dot(
            right_panel.T, jnp.dot(pair_coupling.T, left_proj, precision=HIGH), precision=HIGH
        )
        return first_part - second_part

    coef_inner = jax.vmap(make_coef, in_axes=(0, 0, None, 0, 0, 0))
    new_coef = jax.vmap(coef_inner, in_axes=(0, 0, 0, 0, None, 0))(
        masked_left, masked_right, row_left, coupling, col_left, ortho_basis
    )
    scaled_basis = ortho_basis * math.sqrt(order)
    return (scaled_basis.astype(jnp.bfloat16), new_coef.astype(jnp.bfloat16))


def solution(mesh):
    placed = (
        P(("row", "col"), None),
        P("row", "col", None),
        P("row", "col", None),
        P("row"),
        P("col", "row", None),
        P("col", "row", None),
        P("col"),
        P("row", "col", None, None),
        P("row", "col", None, None),
        P("row", "col"),
    )
    return jax.shard_map(
        body,
        mesh=mesh,
        in_specs=placed,
        out_specs=(P("row", "col", None, None), P("row", "col", None, None)),
        check_vma=False,
    )
```
